512 devices in a mesh: kpt: 16 (over x, y_lo, core), aux: 32 (over z, y_hi).
Axes of the slice: x: 4, y: 4 (y_hi: 2, y_lo: 2; y = y_hi * 2 + y_lo), z: 16, core: 2. Of those that a mesh axis runs over, the one named last changes fastest.
Arguments:
- orbitals: bfloat16 [16, 768, 384], P('kpt', 'aux'), may hold values from -6 to 6
- fitted: bfloat16 [16, 2, 64, 768, 768], P('kpt', None, 'aux'), may hold values from -0.21875 to 0.21875
- kpoint_pair_index: int32 [16, 4], P('kpt'), may hold values from 0 to 1
Outputs:
- exchange_images: float32 [2, 16, 768, 384], P(None, 'kpt', 'aux')
- orbitals_out: float32 [16, 768, 384], P('kpt', 'aux')
The draws below stay inside these ranges and needn't reach their ends.
Inputs may be any that keep to these rules, and one draw needn't show every extreme that they name: kpoint_pair_index[k, v] names which of the 2 fitted tensors of k-point k serves visit v.
All inputs are finite; a program needn't handle non-finite values.
Results may differ from the reference program's by a relative error of at most 0.0011.
Values may be sent and summed in bfloat16 or wider, within the bound.
A program may use at most 64 MiB of HBM per device.

```python
import jax
import jax.numpy as jnp
from jax import lax

BASIS_COUNT = 768
NOCC = 384
SLOT_COUNT = 2
VISIT_COUNT = 4
AUXILIARY_COUNT = 64
KPOINT_COUNT = 16


def with_ends(result, stream_key, least, high):
    index_at = [jax.random.randint(jax.random.fold_in(stream_key, axis), (), 0, length) for axis, length in enumerate(result.shape)]
    main_axis = result.shape.index(max(result.shape))
    neighbour = index_at[:main_axis] + [(index_at[main_axis] + 1) % result.shape[main_axis]] + index_at[main_axis + 1:]
    return result.at[tuple(index_at)].set(least).at[tuple(neighbour)].set(high)


def levels(stream_key, dims, shards, smallest, top_value):
    def one(dim, shards_of):
        heights = jax.random.uniform(jax.random.fold_in(jax.random.fold_in(stream_key, 6), dim), (shards_of,), jnp.float32, smallest / len(shards), top_value / len(shards))
        return jnp.repeat(jnp.exp(heights), dims[dim] // shards_of).reshape((-1,) + (1,) * (len(dims) - dim - 1))

    loudness = one(*shards[0])
    for cut in shards[1:]:
        loudness = loudness * one(*cut)
    return loudness


def bell_draw(own_key, extent, spread, most, cuts=(), kind=jnp.bfloat16):
    result = jax.random.normal(own_key, extent, jnp.float32) * spread
    if len(cuts) > 0:
        result = levels(own_key, extent, cuts, -0.22, 0.18) * result
    return jnp.clip(result, min=-most, max=most).astype(kind)


def setup_inputs(seed: int = 0) -> dict:
    key_of = jax.random.split(jax.random.key(seed), 4)
    return {
        "orbitals": bell_draw(key_of[0], (KPOINT_COUNT, BASIS_COUNT, NOCC), 1.0, 6.0, ((0, 16), (1, 32))),
        "fitted": bell_draw(key_of[1], (KPOINT_COUNT, SLOT_COUNT, AUXILIARY_COUNT, BASIS_COUNT, BASIS_COUNT), BASIS_COUNT ** -0.5, 0.21875, ((0, 16), (2, 32))),
        "kpoint_pair_index": with_ends(jax.random.randint(key_of[2], (KPOINT_COUNT, VISIT_COUNT), 0, SLOT_COUNT), jax.random.fold_in(key_of[2], 1), 0, SLOT_COUNT - 1).astype(jnp.int32),
    }


update_fraction = 0.25


def visit_term(slot_block, paired_kpoint, own_full):
    def accumulate(running, aux_layer):
        half_done = jnp.dot(aux_layer, paired_kpoint, preferred_element_type=jnp.float32).astype(jnp.bfloat16)
        inner_block = jnp.dot(half_done.T, own_full, preferred_element_type=jnp.float32).astype(jnp.bfloat16)
        return running + jnp.dot(half_done, inner_block, preferred_element_type=jnp.float32), None
    running, _ = lax.scan(accumulate, jnp.zeros((BASIS_COUNT, NOCC), jnp.float32), slot_block)
    return running


def reference(orbitals, fitted, kpoint_pair_index):
    current = orbitals.astype(jnp.float32)
    applied_list = []
    norm_scale = 1.0 / (AUXILIARY_COUNT * NOCC)
    for outer in range(VISIT_COUNT // 2):
        offset = outer + 1
        rounded = current.astype(jnp.bfloat16)
        trailing = jnp.roll(rounded, offset, axis=0)
        leading = jnp.roll(rounded, -offset, axis=0)

        def per_point(packed):
            fitted_point, table_row, current_point, trailing_point, leading_point = packed
            slot_first = lax.dynamic_index_in_dim(fitted_point, table_row[2 * outer], 0, keepdims=False)
            slot_second = lax.dynamic_index_in_dim(fitted_point, table_row[2 * outer + 1], 0, keepdims=False)
            running = visit_term(slot_first, trailing_point, current_point)
            running = running + visit_term(slot_second, leading_point, current_point)
            return running * norm_scale

        applied = lax.map(per_point, (fitted, kpoint_pair_index, rounded, trailing, leading))
        applied_list.append(applied)
        current = current - update_fraction * applied
    return jnp.stack(applied_list), current
```

```python
import functools

import jax
import jax.numpy as jnp
from jax import lax
from jax.experimental import pallas as pl
from jax.experimental.pallas import tpu as pltpu
from jax.sharding import PartitionSpec as P

MESH = pl.DeviceIdType.MESH
STEPS = 2
UPDATE = 0.25
PIECES = 3
F32, BF16 = jnp.float32, jnp.bfloat16


def kernel(
    norm,
    orb_ref,
    fit_hbm,
    idx_ref,
    ex_ref,
    out_ref,
    fit,
    pre,
    c48,
    buf,
    xs,
    bt,
    mt,
    part,
    run,
    got,
    ysend,
    yrecv,
    ap,
    fit_sem,
    pre_s,
    pre_r,
    nb_s,
    nb_r,
    ag_s,
    ag_r,
    rs_s,
    rs_r,
    y_s,
    y_r,
):
    k, a = lax.axis_index("kpt"), lax.axis_index("aux")
    nk, na = lax.axis_size("kpt"), lax.axis_size("aux")
    nz = na // 2
    right_hops, left_hops = nz // 2, nz // 2 - 1
    z, h = lax.div(a, 2), lax.rem(a, 2)
    rows, cols = buf.shape[3], buf.shape[4]
    basis = nz * rows
    piece = rows // PIECES

    def dev(dk=0, dz=0, hh=h):
        return (lax.rem(k + dk + nk, nk), lax.rem(z + dz + nz, nz) * 2 + hh)

    fetch = pltpu.make_async_copy(fit_hbm.at[0], fit, fit_sem)
    fetch.start()

    barrier = pltpu.get_barrier_semaphore()
    peers = [dev(dz=1), dev(dz=-1), dev(hh=1 - h)]
    for dk in (1, -1):
        peers += [dev(dk), dev(dk, 0, 1 - h)]
    peers += [dev(2), dev(-2)]
    for peer in peers:
        pl.semaphore_signal(barrier, inc=1, device_id=peer, device_id_type=MESH)
    pl.semaphore_wait(barrier, len(peers))

    def pre_copy(i, slot, target):
        return pltpu.make_async_remote_copy(
            src_ref=orb_ref.at[0],
            dst_ref=pre.at[slot],
            send_sem=pre_s.at[i],
            recv_sem=pre_r.at[slot],
            device_id=target,
            device_id_type=MESH,
        )

    pres = [
        pre_copy(0, 1 + h, dev(1)),
        pre_copy(1, 1 + h, dev(1, 0, 1 - h)),
        pre_copy(2, 3 + h, dev(-1)),
        pre_copy(3, 3 + h, dev(-1, 0, 1 - h)),
        pre_copy(4, 0, dev(hh=1 - h)),
    ]
    for copy in pres:
        copy.start()

    def pre_wait(slot):
        pre_copy(0, slot, dev(1)).wait_recv()

    def ag_copy(t, r, d, s, block):
        return pltpu.make_async_remote_copy(
            src_ref=buf.at[t, r, block],
            dst_ref=buf.at[t, r, block],
            send_sem=ag_s.at[d, t, r, s],
            recv_sem=ag_r.at[d, t, r, s],
            device_id=dev(dz=1 - 2 * d),
            device_id_type=MESH,
        )

    def ag_send(t, r, d, s):
        block = lax.rem(z - s + nz, nz) if d == 0 else lax.rem(z + s, nz)
        return ag_copy(t, r, d, s, block)

    def ag_wait(t, r, d, s):
        block = lax.rem(z - 1 - s + nz, nz) if d == 0 else lax.rem(z + 1 + s, nz)
        ag_copy(t, r, d, s, block).wait_recv()

    def ag_first(t, r):
        ag_send(t, r, 0, 0).start()
        ag_send(t, r, 1, 0).start()

    def ag_relay(t):
        @pl.loop(1, left_hops)
        def _(s):
            for r in range(3):
                ag_wait(t, r, 0, s - 1)
                ag_send(t, r, 0, s).start()
                ag_wait(t, r, 1, s - 1)
                ag_send(t, r, 1, s).start()

        for r in range(3):
            ag_wait(t, r, 0, right_hops - 2)
            ag_send(t, r, 0, right_hops - 1).start()

    def ag_last(t, r):
        ag_wait(t, r, 1, left_hops - 1)
        ag_wait(t, r, 0, right_hops - 1)

    def rs_copy(t, d, s, c, src):
        return pltpu.make_async_remote_copy(
            src_ref=src,
            dst_ref=got.at[t, d, s, c],
            send_sem=rs_s.at[d, t, s, c],
            recv_sem=rs_r.at[d, t, s, c],
            device_id=dev(dz=1 - 2 * d),
            device_id_type=MESH,
        )

    def rs_target(d, s):
        if d == 0:
            return lax.rem(z + right_hops - s, nz)
        return lax.rem(z - left_hops + s + nz, nz)

    def rs_first(t):
        for c in range(PIECES):
            for d in range(2):
                rs_copy(t, d, 0, c, part.at[t, rs_target(d, 0), c]).start()

    def rs_step(t, d, s, c):
        rs_copy(t, d, s - 1, c, run.at[t, d, s - 1, c]).wait_recv()
        run[t, d, s, c] = part[t, rs_target(d, s), c] + got[t, d, s - 1, c]
        rs_copy(t, d, s, c, run.at[t, d, s, c]).start()

    def y_copy(t, c):
        return pltpu.make_async_remote_copy(
            src_ref=ysend.at[t, c],
            dst_ref=yrecv.at[t, c],
            send_sem=y_s.at[t, c],
            recv_sem=y_r.at[t, c],
            device_id=dev(hh=1 - h),
            device_id_type=MESH,
        )

    def reduce(t):
        @pl.loop(1, left_hops)
        def _(s):
            for c in range(PIECES):
                for d in range(2):
                    rs_step(t, d, s, c)

        for c in range(PIECES):
            rs_step(t, 0, right_hops - 1, c)
        for c in range(PIECES):
            rs_copy(t, 1, left_hops - 1, c, run.at[t, 1, left_hops - 1, c]).wait_recv()
            rs_copy(t, 0, right_hops - 1, c, run.at[t, 0, right_hops - 1, c]).wait_recv()
            ysend[t, c] = (
                part[t, z, c]
                + got[t, 1, left_hops - 1, c]
                + got[t, 0, right_hops - 1, c]
            )
            y_copy(t, c).start()
        for c in range(PIECES):
            y_copy(t, c).wait_recv()
        total = (ysend[t] + yrecv[t]) * norm
        return total.reshape(2, rows // 2, cols)

    def nb_copy(i, r, target):
        return pltpu.make_async_remote_copy(
            src_ref=buf.at[1, 2, z],
            dst_ref=buf.at[1, r, z],
            send_sem=nb_s.at[i],
            recv_sem=nb_r.at[i],
            device_id=target,
            device_id_type=MESH,
        )

    tall = 256
    for t in range(STEPS):
        if t == 0:
            for r in range(2):
                pre_wait(1 + 2 * r)
                pre_wait(2 + 2 * r)
                both = pre[1 + 2 * r : 3 + 2 * r].astype(F32)
                buf[0, r, z] = both.reshape(rows, cols).astype(BF16)
                ag_first(0, r)
            pre_wait(0)
            c48[h] = orb_ref[0].astype(F32)
            c48[1 - h] = pre[0].astype(F32)
            buf[0, 2, z] = c48[...].reshape(rows, cols).astype(BF16)
            ag_first(0, 2)
        else:
            buf[1, 2, z] = c48[...].reshape(rows, cols).astype(BF16)
            ups = [nb_copy(0, 0, dev(2)), nb_copy(1, 1, dev(-2))]
            for copy in ups:
                copy.start()
            ag_first(1, 2)
            for r in range(2):
                ups[r].wait_recv()
                ag_first(1, r)
        ag_relay(t)
        if t == 0:
            fetch.wait()
        for v in range(2):
            ag_last(t, v)
            slot = idx_ref[0, 2 * t + v]
            for p in range(2):

                @pl.loop(0, basis // tall)
                def _(i):
                    x = jnp.dot(
                        fit[slot, p, pl.ds(i * tall, tall), :],
                        buf[t, v].reshape(basis, cols),
                        preferred_element_type=F32,
                    )
                    at = (2 * v + p) * cols
                    xs[pl.ds(i * tall, tall), at : at + cols] = x.astype(BF16)

        ag_last(t, 2)
        bt[...] = buf[t, 2].reshape(basis, cols).T
        for n in range(4):
            mt[:, n * cols : (n + 1) * cols] = jnp.dot(
                bt[...], xs[:, n * cols : (n + 1) * cols], preferred_element_type=F32
            ).astype(BF16)

        @pl.loop(0, 4)
        def _(i):
            y = lax.dot_general(
                xs[pl.ds(i * (basis // 4), basis // 4), :],
                mt[...],
                (((1,), (1,)), ((), ())),
                preferred_element_type=F32,
            )
            part[t, pl.ds(i * (nz // 4), nz // 4)] = y.reshape(
                nz // 4, PIECES, piece, cols
            )

        rs_first(t)
        applied = reduce(t)
        ap[...] = applied
        c48[...] = c48[...] - UPDATE * applied
        ex_ref[t, 0] = ap[h]
    out_ref[0] = c48[h]

    for i, copy in enumerate(pres):
        copy.wait_send()
    for copy in ups:
        copy.wait_send()
    for t in range(STEPS):
        for c in range(PIECES):
            y_copy(t, c).wait_send()

        @pl.loop(0, left_hops)
        def _(s):
            for d in range(2):
                for r in range(3):
                    ag_send(t, r, d, s).wait_send()
                for c in range(PIECES):
                    rs_copy(t, d, s, c, run.at[t, d, s, c]).wait_send()

        for r in range(3):
            ag_send(t, r, 0, right_hops - 1).wait_send()
        for c in range(PIECES):
            rs_copy(t, 0, right_hops - 1, c, run.at[t, 0, right_hops - 1, c]).wait_send()


def on_device(orbitals, fitted, kpoint_pair_index):
    _, half, cols = orbitals.shape
    _, slots, layers, basis, _ = fitted.shape
    na = lax.axis_size("aux")
    nz, rows = na // 2, 2 * half
    hops = nz // 2
    piece = rows // PIECES
    norm = 1.0 / (layers * na * cols)
    vmem = functools.partial(pl.BlockSpec, memory_space=pltpu.VMEM)
    dma = pltpu.SemaphoreType.DMA
    return pl.pallas_call(
        functools.partial(kernel, norm),
        out_shape=(
            jax.ShapeDtypeStruct((STEPS, 1, half, cols), F32),
            jax.ShapeDtypeStruct((1, half, cols), F32),
        ),
        in_specs=[
            vmem(),
            pl.BlockSpec(memory_space=pl.ANY),
            pl.BlockSpec(memory_space=pltpu.SMEM),
        ],
        out_specs=(vmem(), vmem()),
        scratch_shapes=[
            pltpu.VMEM((slots, layers, basis, basis), BF16),
            pltpu.VMEM((5, half, cols), BF16),
            pltpu.VMEM((2, half, cols), F32),
            pltpu.VMEM((STEPS, 3, nz, rows, cols), BF16),
            pltpu.VMEM((basis, 4 * cols), BF16),
            pltpu.VMEM((cols, basis), BF16),
            pltpu.VMEM((cols, 4 * cols), BF16),
            pltpu.VMEM((STEPS, nz, PIECES, piece, cols), F32),
            pltpu.VMEM((STEPS, 2, hops, PIECES, piece, cols), F32),
            pltpu.VMEM((STEPS, 2, hops, PIECES, piece, cols), F32),
            pltpu.VMEM((STEPS, PIECES, piece, cols), F32),
            pltpu.VMEM((STEPS, PIECES, piece, cols), F32),
            pltpu.VMEM((2, half, cols), F32),
            dma,
            dma((5,)),
            dma((5,)),
            dma((2,)),
            dma((2,)),
            dma((2, STEPS, 3, hops)),
            dma((2, STEPS, 3, hops)),
            dma((2, STEPS, hops, PIECES)),
            dma((2, STEPS, hops, PIECES)),
            dma((STEPS, PIECES)),
            dma((STEPS, PIECES)),
        ],
        compiler_params=pltpu.CompilerParams(
            collective_id=0, has_side_effects=True, vmem_limit_bytes=56 * 2**20
        ),
        name="exchange",
    )(orbitals, fitted, kpoint_pair_index)


def solution(mesh):
    placed = (P("kpt", "aux", None), P("kpt", None, "aux", None, None), P("kpt", None))
    return jax.shard_map(
        on_device,
        mesh=mesh,
        in_specs=placed,
        out_specs=(P(None, "kpt", "aux", None), P("kpt", "aux", None)),
        check_vma=False,
    )
```

```python
import functools

import jax
import jax.numpy as jnp
from jax import lax
from jax.experimental import pallas as pl
from jax.experimental.pallas import tpu as pltpu
from jax.sharding import PartitionSpec as P

MESH = pl.DeviceIdType.MESH
STEPS = 2
UPDATE = 0.25
PIECES = 3
F32, BF16 = jnp.float32, jnp.bfloat16
GATHER_RELAYS = (0, 2, 4, 6)
REDUCE_RELAYS = (0, 2, 4, 6)


def parent(relays, distance):
    return max(r for r in relays if r < distance)


def kernel(
    norm,
    orb_ref,
    fit_hbm,
    idx_ref,
    tot_ref,
    fit,
    pre,
    c48,
    buf,
    xs,
    bt,
    mt,
    part,
    run,
    got,
    ysend,
    yrecv,
    ap,
    fit_sem,
    pre_s,
    pre_r,
    nb_s,
    nb_r,
    ag_s,
    ag_r,
    rs_s,
    rs_r,
    y_s,
    y_r,
):
    k, a = lax.axis_index("kpt"), lax.axis_index("aux")
    nk, na = lax.axis_size("kpt"), lax.axis_size("aux")
    nz = na // 2
    far = (nz // 2, nz // 2 - 1)
    z, h = lax.div(a, 2), lax.rem(a, 2)
    rows, cols = buf.shape[3], buf.shape[4]
    basis = nz * rows
    piece = rows // PIECES

    def dev(dk=0, dz=0, hh=h):
        return (lax.rem(k + dk + nk, nk), lax.rem(z + dz + nz, nz) * 2 + hh)

    def place(d, distance):
        return lax.rem(z + (1 - 2 * d) * distance + nz, nz)

    def slot_of(d, distance):
        return d * far[0] + distance - 1

    fetch = pltpu.make_async_copy(fit_hbm.at[0], fit, fit_sem)
    fetch.start()

    barrier = pltpu.get_barrier_semaphore()
    peers = [dev(hh=1 - h)] + [dev(dz=dz) for dz in (1, -1, 2, -2)]
    for dk in (1, -1, 2, -2):
        peers += [dev(dk), dev(dk, 0, 1 - h)]
    for peer in peers:
        pl.semaphore_signal(barrier, inc=1, device_id=peer, device_id_type=MESH)
    pl.semaphore_wait(barrier, len(peers))

    def remote(src, dst, send_sem, recv_sem, target):
        return pltpu.make_async_remote_copy(
            src_ref=src,
            dst_ref=dst,
            send_sem=send_sem,
            recv_sem=recv_sem,
            device_id=target,
            device_id_type=MESH,
        )

    first = remote(orb_ref.at[0], pre, pre_s, pre_r, dev(hh=1 - h))
    first.start()

    def hand(t, block):
        other = lax.rem(h + block, 2)
        src = buf.at[t, 2, block]
        for r, dk in ((0, t + 1), (1, -t - 1)):
            remote(
                src, buf.at[t, r, block], nb_s.at[t], nb_r.at[t, r], dev(dk, 0, other)
            ).start()

    def ag_send(t, d, block, at, to):
        ref = buf.at[t, 2, block]
        remote(
            ref,
            ref,
            ag_s.at[t],
            ag_r.at[t, slot_of(d, to)],
            dev(dz=(1 - 2 * d) * (to - at)),
        ).start()

    def ag_relay(t, d, at):
        block = place(1 - d, at)
        for to in range(far[d], at, -1):
            if parent(GATHER_RELAYS, to) == at:
                ag_send(t, d, block, at, to)

    def ag_wait(t, d, at):
        ref = buf.at[t, 2, place(1 - d, at)]
        remote(ref, ref, ag_s.at[t], ag_r.at[t, slot_of(d, at)], dev(dz=1)).wait_recv()

    def gather(t):
        for d in range(2):
            ag_relay(t, d, 0)
        hand(t, z)
        last = 0
        for at in GATHER_RELAYS[1:] + (far[0],):
            for d in range(2):
                if at <= far[d]:
                    ag_wait(t, d, at)
                    if at in GATHER_RELAYS:
                        ag_relay(t, d, at)
            for between in range(last + 1, at):
                for d in range(2):
                    ag_wait(t, d, between)
                    hand(t, place(1 - d, between))
            for d in range(2):
                if at <= far[d]:
                    hand(t, place(1 - d, at))
            last = at

    def nb_wait(t, r):
        ref = buf.at[t, r]
        remote(ref, ref, nb_s.at[t], nb_r.at[t, r], dev(1)).wait_recv()

    def rs_copy(t, d, at, c, src):
        to = parent(REDUCE_RELAYS, at)
        i = slot_of(d, at)
        return remote(
            src,
            got.at[t, i, c],
            rs_s.at[t],
            rs_r.at[t, i, c],
            dev(dz=(1 - 2 * d) * (at - to)),
        )

    def rs_leaf(t, at):
        for c in range(PIECES):
            for d in range(2):
                if at <= far[d]:
                    rs_copy(t, d, at, c, part.at[t, place(d, at), c]).start()

    def rs_sum(t, d, at, c):
        total = part[t, place(d, at), c]
        for child in range(far[d], at, -1):
            if parent(REDUCE_RELAYS, child) == at:
                i = slot_of(d, child)
                rs_copy(t, d, child, c, got.at[t, i, c]).wait_recv()
                total = total + got[t, i, c]
        return total

    def rs_relay(t, at):
        i = REDUCE_RELAYS.index(at) - 1

        @pl.loop(0, PIECES)
        def _(c):
            for d in range(2):
                run[t, d, i, c] = rs_sum(t, d, at, c)
                rs_copy(t, d, at, c, run.at[t, d, i, c]).start()

    def y_copy(t, c):
        return remote(
            ysend.at[t, c], yrecv.at[t, c], y_s.at[t], y_r.at[t, c], dev(hh=1 - h)
        )

    def reduce(t):
        for at in REDUCE_RELAYS[:0:-1]:
            rs_relay(t, at)
            if at - 3 > 0 and at - 3 not in REDUCE_RELAYS:
                rs_leaf(t, at - 3)

        @pl.loop(0, PIECES)
        def _(c):
            total = rs_sum(t, 0, 0, c)
            for child in range(far[1], 0, -1):
                if parent(REDUCE_RELAYS, child) == 0:
                    i = slot_of(1, child)
                    rs_copy(t, 1, child, c, got.at[t, i, c]).wait_recv()
                    total = total + got[t, i, c]
            ysend[t, c] = total
            y_copy(t, c).start()

        for c in range(PIECES):
            y_copy(t, c).wait_recv()
        return (ysend[t] + yrecv[t]).reshape(2, rows // 2, cols)

    tall = 256
    group = nz // 4
    for t in range(STEPS):
        if t == 0:
            first.wait_recv()
            c48[h] = orb_ref[0].astype(F32)
            c48[1 - h] = pre[...].astype(F32)
        buf[t, 2, z] = c48[...].reshape(rows, cols).astype(BF16)
        gather(t)
        bt[...] = buf[t, 2].reshape(basis, cols).T
        if t == 0:
            fetch.wait()
        for v in range(2):
            nb_wait(t, v)
            slot = idx_ref[0, 2 * t + v]
            for p in range(2):

                @pl.loop(0, basis // tall)
                def _(i):
                    x = jnp.dot(
                        fit[slot, p, pl.ds(i * tall, tall), :],
                        buf[t, v].reshape(basis, cols),
                        preferred_element_type=F32,
                    )
                    at = (2 * v + p) * cols
                    xs[pl.ds(i * tall, tall), at : at + cols] = x.astype(BF16)

        for n in range(4):
            mt[:, n * cols : (n + 1) * cols] = jnp.dot(
                bt[...], xs[:, n * cols : (n + 1) * cols], preferred_element_type=F32
            ).astype(BF16)

        home = lax.div(z, group) + 2
        side = jnp.where(lax.rem(z, group) * 2 >= group, 1, 3)

        def tile(i):
            y = lax.dot_general(
                xs[pl.ds(pl.multiple_of(i * (basis // 4), basis // 4), basis // 4), :],
                mt[...],
                (((1,), (1,)), ((), ())),
                preferred_element_type=F32,
            )
            part[t, pl.ds(i * group, group)] = y.reshape(group, PIECES, piece, cols)

        @pl.loop(0, 2)
        def _(i):
            tile(lax.rem(home + i * side, 4))

        rs_leaf(t, 8)
        rs_leaf(t, 7)

        @pl.loop(0, 2)
        def _(i):
            tile(lax.rem(home + 2 + i * side, 4))

        rs_leaf(t, 5)
        total = reduce(t)
        ap[...] = total
        tot_ref[t] = ap[h]
        if t < STEPS - 1:
            c48[...] = c48[...] - UPDATE * (total * norm)

    first.wait_send()
    for t in range(STEPS):
        y_all = ysend.at[t]
        remote(y_all, y_all, y_s.at[t], y_r.at[t, 0], dev(1)).wait_send()
        ring = buf.at[t, 2, pl.ds(0, nz - 1)]
        remote(ring, ring, ag_s.at[t], ag_r.at[t, 0], dev(1)).wait_send()
        handed = buf.at[t, pl.ds(0, 2)]
        remote(handed, handed, nb_s.at[t], nb_r.at[t, 0], dev(1)).wait_send()
        summed = got.at[t]
        remote(summed, summed, rs_s.at[t], rs_r.at[t, 0, 0], dev(1)).wait_send()


def on_device(orbitals, fitted, kpoint_pair_index):
    _, half, cols = orbitals.shape
    _, slots, layers, basis, _ = fitted.shape
    na = lax.axis_size("aux")
    nz, rows = na // 2, 2 * half
    piece = rows // PIECES
    norm = 1.0 / (layers * na * cols)
    relays = len(REDUCE_RELAYS) - 1
    vmem = functools.partial(pl.BlockSpec, memory_space=pltpu.VMEM)
    dma = pltpu.SemaphoreType.DMA
    totals = pl.pallas_call(
        functools.partial(kernel, norm),
        out_shape=jax.ShapeDtypeStruct((STEPS, half, cols), F32),
        in_specs=[
            vmem(),
            pl.BlockSpec(memory_space=pl.ANY),
            pl.BlockSpec(memory_space=pltpu.SMEM),
        ],
        out_specs=vmem(),
        scratch_shapes=[
            pltpu.VMEM((slots, layers, basis, basis), BF16),
            pltpu.VMEM((half, cols), BF16),
            pltpu.VMEM((2, half, cols), F32),
            pltpu.VMEM((STEPS, 3, nz, rows, cols), BF16),
            pltpu.VMEM((basis, 4 * cols), BF16),
            pltpu.VMEM((cols, basis), BF16),
            pltpu.VMEM((cols, 4 * cols), BF16),
            pltpu.VMEM((STEPS, nz, PIECES, piece, cols), F32),
            pltpu.VMEM((STEPS, 2, relays, PIECES, piece, cols), F32),
            pltpu.VMEM((STEPS, nz - 1, PIECES, piece, cols), F32),
            pltpu.VMEM((STEPS, PIECES, piece, cols), F32),
            pltpu.VMEM((STEPS, PIECES, piece, cols), F32),
            pltpu.VMEM((2, half, cols), F32),
            dma,
            dma,
            dma,
            dma((STEPS,)),
            dma((STEPS, 2)),
            dma((STEPS,)),
            dma((STEPS, nz - 1)),
            dma((STEPS,)),
            dma((STEPS, nz - 1, PIECES)),
            dma((STEPS,)),
            dma((STEPS, PIECES)),
        ],
        compiler_params=pltpu.CompilerParams(
            collective_id=0, has_side_effects=True, vmem_limit_bytes=56 * 2**20
        ),
        name="exchange",
    )(orbitals, fitted, kpoint_pair_index)
    applied = totals * norm
    current = orbitals[0].astype(F32)
    for t in range(STEPS):
        current = current - UPDATE * applied[t]
    return applied[:, None], current[None]


def solution(mesh):
    placed = (P("kpt", "aux", None), P("kpt", None, "aux", None, None), P("kpt", None))
    return jax.shard_map(
        on_device,
        mesh=mesh,
        in_specs=placed,
        out_specs=(P(None, "kpt", "aux", None), P("kpt", "aux", None)),
        check_vma=False,
    )
```

```python
import functools

import jax
import jax.numpy as jnp
from jax import lax
from jax.experimental import pallas as pl
from jax.experimental.pallas import tpu as pltpu
from jax.sharding import PartitionSpec as P

MESH = pl.DeviceIdType.MESH
STEPS = 2
UPDATE = 0.25
PIECES = 3
F32, BF16 = jnp.float32, jnp.bfloat16
GATHER_RELAYS = (0, 3, 6)
REDUCE_RELAYS = (0, 2, 4, 6)
PEER_Z = (1, -1, 2, -2, 3, -3)


def parent(relays, distance):
    return max(r for r in relays if r < distance)


def kernel(
    norm,
    orb_ref,
    fit_hbm,
    idx_ref,
    tot_ref,
    fit,
    pre,
    c48,
    buf,
    xs,
    bt,
    mt,
    part,
    run,
    got,
    ysend,
    yrecv,
    ap,
    fit_sem,
    pre_s,
    pre_r,
    nb_s,
    nb_r,
    ag_s,
    ag_r,
    rs_s,
    rs_r,
    y_s,
    y_r,
):
    k, a = lax.axis_index("kpt"), lax.axis_index("aux")
    nk, na = lax.axis_size("kpt"), lax.axis_size("aux")
    nz = na // 2
    half = nz // 2
    far = half - 1
    z, h = lax.div(a, 2), lax.rem(a, 2)
    odd = lax.rem(z, 2)
    piece, cols = buf.shape[4], buf.shape[5]
    rows = PIECES * piece
    basis = nz * rows

    def dev(dk=0, dz=0, hh=h):
        return (lax.rem(k + dk + nk, nk), lax.rem(z + dz + nz, nz) * 2 + hh)

    def place(d, distance):
        return lax.rem(z + (1 - 2 * d) * distance + nz, nz)

    def slot_of(d, distance):
        return nz - 2 if distance == half else d * far + distance - 1

    fetch = pltpu.make_async_copy(fit_hbm.at[0], fit, fit_sem)
    fetch.start()

    barrier = pltpu.get_barrier_semaphore()
    peers = [dev(hh=1 - h)] + [dev(dz=dz) for dz in PEER_Z]
    for dk in (1, -1, 2, -2):
        peers += [dev(dk), dev(dk, 0, 1 - h)]
    for peer in peers:
        pl.semaphore_signal(barrier, inc=1, device_id=peer, device_id_type=MESH)
    pl.semaphore_wait(barrier, len(peers))

    def remote(src, dst, send_sem, recv_sem, target):
        return pltpu.make_async_remote_copy(
            src_ref=src,
            dst_ref=dst,
            send_sem=send_sem,
            recv_sem=recv_sem,
            device_id=target,
            device_id_type=MESH,
        )

    first = remote(orb_ref.at[0], pre, pre_s, pre_r, dev(hh=1 - h))
    first.start()

    def hand(t, block):
        src = buf.at[t, 2, block]
        for r, dk in ((0, t + 1), (1, -t - 1)):
            other = lax.rem(h + block, 2)
            if t == 0:
                other = jnp.where(lax.rem(k + r, 2) == 0, h, other)
            remote(
                src, buf.at[t, r, block], nb_s.at[t], nb_r.at[t, r], dev(dk, 0, other)
            ).start()

    def ag_edge(t, d, block, at, to, c=None):
        ref = buf.at[t, 2, block]
        whole = to not in GATHER_RELAYS
        i = slot_of(d, to)
        return remote(
            ref if whole else ref.at[c],
            ref if whole else ref.at[c],
            ag_s.at[t],
            ag_r.at[t, i, 0 if whole else c],
            dev(dz=(1 - 2 * d) * (to - at)),
        )

    def ag_pass(t, d, at, c):
        for to in GATHER_RELAYS:
            if to > at and parent(GATHER_RELAYS, to) == at:
                ag_edge(t, d, place(1 - d, at), at, to, c).start()

    def ag_leaves(t, d, at):
        for to in range(far, at, -1):
            if parent(GATHER_RELAYS, to) == at and to not in GATHER_RELAYS:
                ag_edge(t, d, place(1 - d, at), at, to).start()

    def ag_wait(t, d, at, c=None):
        ag_edge(t, d, place(1 - d, at), 0, at, c).wait_recv()

    def gather(t):
        last = 0
        for at in GATHER_RELAYS:
            if at > 0:

                @pl.loop(0, PIECES)
                def _(c):
                    for d in range(2):
                        ag_wait(t, d, at, c)
                        ag_pass(t, d, at, c)

            if at == GATHER_RELAYS[-1]:
                ag_edge(t, odd, place(1 - odd, at), at, half).start()
            for d in range(2):
                ag_leaves(t, d, at)
            for between in range(last + 1, at):
                for d in range(2):
                    ag_wait(t, d, between)
                    hand(t, place(1 - d, between))
            for d in range(2 if at > 0 else 1):
                hand(t, place(1 - d, at))
            last = at
        for between in range(last + 1, half):
            for d in range(2):
                ag_wait(t, d, between)
                hand(t, place(1 - d, between))
        ag_wait(t, 0, half)
        hand(t, place(0, half))

    def nb_wait(t, r):
        ref = buf.at[t, r]
        remote(ref, ref, nb_s.at[t], nb_r.at[t, r], dev(1)).wait_recv()

    def rs_copy(t, d, at, c, src):
        to = parent(REDUCE_RELAYS, at)
        i = slot_of(d, at)
        return remote(
            src,
            got.at[t, i, c],
            rs_s.at[t],
            rs_r.at[t, i, c],
            dev(dz=(1 - 2 * d) * (at - to)),
        )

    def rs_leaves(t, group):
        for c in range(PIECES):
            for at in group:
                if at == half:
                    rs_copy(t, odd, at, c, part.at[t, place(0, at), c]).start()
                else:
                    for d in range(2):
                        rs_copy(t, d, at, c, part.at[t, place(d, at), c]).start()

    leaves = [
        [at for at in range(half, 0, -1) if parent(REDUCE_RELAYS, at) == relay
         and at not in REDUCE_RELAYS]
        for relay in REDUCE_RELAYS[::-1]
    ]

    def rs_sum(t, d, at, c):
        total = part[t, place(d, at), c]
        for child in range(far, at, -1):
            if parent(REDUCE_RELAYS, child) == at:
                i = slot_of(d, child)
                rs_copy(t, d, child, c, got.at[t, i, c]).wait_recv()
                total = total + got[t, i, c]
        return total

    def rs_relay(t, at):
        i = REDUCE_RELAYS.index(at) - 1

        @pl.loop(0, PIECES)
        def _(c):
            sums = [rs_sum(t, d, at, c) for d in range(2)]
            if at == REDUCE_RELAYS[-1]:
                opposite = got.at[t, nz - 2, c]
                rs_copy(t, 0, half, c, opposite).wait_recv()
                add = opposite[...]
                none = jnp.zeros_like(add)
                sums[0] = sums[0] + jnp.where(odd == 0, add, none)
                sums[1] = sums[1] + jnp.where(odd == 1, add, none)
            for d in range(2):
                run[t, d, i, c] = sums[d]
                rs_copy(t, d, at, c, run.at[t, d, i, c]).start()

    def y_copy(t, c):
        return remote(
            ysend.at[t, c], yrecv.at[t, c], y_s.at[t], y_r.at[t, c], dev(hh=1 - h)
        )

    def reduce(t):
        for n, at in enumerate(REDUCE_RELAYS[:0:-1]):
            rs_relay(t, at)
            for leaf in leaves[n + 2 : n + 3]:
                rs_leaves(t, leaf)

        @pl.loop(0, PIECES)
        def _(c):
            total = rs_sum(t, 0, 0, c)
            for child in range(far, 0, -1):
                if parent(REDUCE_RELAYS, child) == 0:
                    i = slot_of(1, child)
                    rs_copy(t, 1, child, c, got.at[t, i, c]).wait_recv()
                    total = total + got[t, i, c]
            ysend[t, c] = total
            y_copy(t, c).start()

        @pl.loop(0, PIECES)
        def _(c):
            y_copy(t, c).wait_recv()
            total = ysend[t, c] + yrecv[t, c]
            here = pl.ds(pl.multiple_of(c * piece, piece), piece)
            ap[here, :] = total
            if t < STEPS - 1:
                fresh = c48[here, :] - UPDATE * (total * norm)
                c48[here, :] = fresh
                start(t + 1, c, fresh)

    def start(t, c, fresh):
        buf[t, 2, z, c] = fresh.astype(BF16)
        for d in range(2):
            ag_pass(t, d, 0, c)

    def half_of(which):
        return pl.ds(pl.multiple_of(which * (rows // 2), 8), rows // 2)

    tall = 256
    group = nz // 4
    for t in range(STEPS):
        if t == 0:
            first.wait_recv()
            c48[half_of(h), :] = orb_ref[0].astype(F32)
            c48[half_of(1 - h), :] = pre[...].astype(F32)
            for c in range(PIECES):
                start(0, c, c48[c * piece : (c + 1) * piece, :])
        gather(t)
        bt[...] = buf[t, 2].reshape(basis, cols).T
        if t == 0:
            fetch.wait()
        near = 1 - lax.rem(lax.div(k, t + 1), 2)
        for n in range(2):
            v = near if n == 0 else 1 - near
            nb_wait(t, v)
            slot = idx_ref[0, 2 * t + v]
            for p in range(2):

                @pl.loop(0, basis // tall)
                def _(i):
                    x = jnp.dot(
                        fit[slot, p, pl.ds(i * tall, tall), :],
                        buf[t, v].reshape(basis, cols),
                        preferred_element_type=F32,
                    )
                    at = (2 * n + p) * cols
                    xs[pl.ds(i * tall, tall), at : at + cols] = x.astype(BF16)

            for m in (2 * n, 2 * n + 1):
                at = m * cols
                mt[:, at : at + cols] = jnp.dot(
                    bt[...], xs[:, at : at + cols], preferred_element_type=F32
                ).astype(BF16)

        home = lax.div(z, group) + 2
        side = jnp.where(lax.rem(z, group) * 2 >= group, 1, 3)

        def tile(i):
            y = lax.dot_general(
                xs[pl.ds(pl.multiple_of(i * (basis // 4), basis // 4), basis // 4), :],
                mt[...],
                (((1,), (1,)), ((), ())),
                preferred_element_type=F32,
            )
            part[t, pl.ds(i * group, group)] = y.reshape(group, PIECES, piece, cols)

        @pl.loop(0, 2)
        def _(i):
            tile(lax.rem(home + i * side, 4))

        rs_leaves(t, leaves[0])

        @pl.loop(0, 2)
        def _(i):
            tile(lax.rem(home + 2 + i * side, 4))

        rs_leaves(t, leaves[1])
        reduce(t)
        tot_ref[t] = ap[half_of(h), :]

    first.wait_send()
    for t in range(STEPS):
        y_all = ysend.at[t]
        remote(y_all, y_all, y_s.at[t], y_r.at[t, 0], dev(1)).wait_send()
        ring = buf.at[t, 2, pl.ds(0, nz - 1)]
        remote(ring, ring, ag_s.at[t], ag_r.at[t, 0, 0], dev(1)).wait_send()
        handed = buf.at[t, pl.ds(0, 2)]
        remote(handed, handed, nb_s.at[t], nb_r.at[t, 0], dev(1)).wait_send()
        summed = got.at[t]
        remote(summed, summed, rs_s.at[t], rs_r.at[t, 0, 0], dev(1)).wait_send()


def finish(norm, tot_ref, orb_ref, ex_ref, out_ref):
    current = orb_ref[0].astype(F32)
    for t in range(STEPS):
        applied = tot_ref[t] * norm
        ex_ref[t, 0] = applied
        current = current - UPDATE * applied
    out_ref[0] = current


def on_device(orbitals, fitted, kpoint_pair_index):
    _, half, cols = orbitals.shape
    _, slots, layers, basis, _ = fitted.shape
    na = lax.axis_size("aux")
    nz, rows = na // 2, 2 * half
    piece = rows // PIECES
    norm = 1.0 / (layers * na * cols)
    relays = len(REDUCE_RELAYS) - 1
    vmem = functools.partial(pl.BlockSpec, memory_space=pltpu.VMEM)
    dma = pltpu.SemaphoreType.DMA
    totals = pl.pallas_call(
        functools.partial(kernel, norm),
        out_shape=jax.ShapeDtypeStruct((STEPS, half, cols), F32),
        in_specs=[
            vmem(),
            pl.BlockSpec(memory_space=pl.ANY),
            pl.BlockSpec(memory_space=pltpu.SMEM),
        ],
        out_specs=vmem(),
        scratch_shapes=[
            pltpu.VMEM((slots, layers, basis, basis), BF16),
            pltpu.VMEM((half, cols), BF16),
            pltpu.VMEM((rows, cols), F32),
            pltpu.VMEM((STEPS, 3, nz, PIECES, piece, cols), BF16),
            pltpu.VMEM((basis, 4 * cols), BF16),
            pltpu.VMEM((cols, basis), BF16),
            pltpu.VMEM((cols, 4 * cols), BF16),
            pltpu.VMEM((STEPS, nz, PIECES, piece, cols), F32),
            pltpu.VMEM((STEPS, 2, relays, PIECES, piece, cols), F32),
            pltpu.VMEM((STEPS, nz - 1, PIECES, piece, cols), F32),
            pltpu.VMEM((STEPS, PIECES, piece, cols), F32),
            pltpu.VMEM((STEPS, PIECES, piece, cols), F32),
            pltpu.VMEM((rows, cols), F32),
            dma,
            dma,
            dma,
            dma((STEPS,)),
            dma((STEPS, 2)),
            dma((STEPS,)),
            dma((STEPS, nz - 1, PIECES)),
            dma((STEPS,)),
            dma((STEPS, nz - 1, PIECES)),
            dma((STEPS,)),
            dma((STEPS, PIECES)),
        ],
        compiler_params=pltpu.CompilerParams(
            collective_id=0, has_side_effects=True, vmem_limit_bytes=56 * 2**20
        ),
        name="exchange",
    )(orbitals, fitted, kpoint_pair_index)
    return pl.pallas_call(
        functools.partial(finish, norm),
        out_shape=(
            jax.ShapeDtypeStruct((STEPS, 1, half, cols), F32),
            jax.ShapeDtypeStruct((1, half, cols), F32),
        ),
        in_specs=[vmem(), vmem()],
        out_specs=(vmem(), vmem()),
        name="finish",
    )(totals, orbitals)


def solution(mesh):
    placed = (P("kpt", "aux", None), P("kpt", None, "aux", None, None), P("kpt", None))
    return jax.shard_map(
        on_device,
        mesh=mesh,
        in_specs=placed,
        out_specs=(P(None, "kpt", "aux", None), P("kpt", "aux", None)),
        check_vma=False,
    )
```

```python
import functools

import jax
import jax.numpy as jnp
from jax import lax
from jax.experimental import pallas as pl
from jax.experimental.pallas import tpu as pltpu
from jax.sharding import PartitionSpec as P

MESH = pl.DeviceIdType.MESH
STEPS = 2
UPDATE = 0.25
PIECES = 3
F32, BF16 = jnp.float32, jnp.bfloat16
GATHER_RELAYS = (0, 3, 6)
REDUCE_RELAYS = (0, 2, 4, 6)
PEER_Z = (1, -1, 2, -2, 3, -3)


def parent(relays, distance):
    return max(r for r in relays if r < distance)


def kernel(
    norm,
    orb_ref,
    fit_hbm,
    idx_ref,
    tot_ref,
    fit,
    pre,
    c48,
    buf,
    xs,
    bt,
    mt,
    part,
    run,
    got,
    ysend,
    yrecv,
    ap,
    fit_sem,
    pre_s,
    pre_r,
    nb_s,
    nb_r,
    ag_s,
    ag_r,
    rs_s,
    rs_r,
    y_s,
    y_r,
):
    k, a = lax.axis_index("kpt"), lax.axis_index("aux")
    nk, na = lax.axis_size("kpt"), lax.axis_size("aux")
    nz = na // 2
    half = nz // 2
    far = half - 1
    z, h = lax.div(a, 2), lax.rem(a, 2)
    odd = lax.rem(z, 2)
    piece, cols = buf.shape[4], buf.shape[5]
    rows = PIECES * piece
    basis = nz * rows

    def dev(dk=0, dz=0, hh=h):
        return (lax.rem(k + dk + nk, nk), lax.rem(z + dz + nz, nz) * 2 + hh)

    def place(d, distance):
        return lax.rem(z + (1 - 2 * d) * distance + nz, nz)

    def slot_of(d, distance):
        return nz - 2 if distance == half else d * far + distance - 1

    fetch = pltpu.make_async_copy(fit_hbm.at[0], fit, fit_sem)
    fetch.start()

    barrier = pltpu.get_barrier_semaphore()
    peers = [dev(hh=1 - h)] + [dev(dz=dz) for dz in PEER_Z]
    for dk in (1, -1, 2, -2):
        peers += [dev(dk), dev(dk, 0, 1 - h)]
    for peer in peers:
        pl.semaphore_signal(barrier, inc=1, device_id=peer, device_id_type=MESH)
    pl.semaphore_wait(barrier, len(peers))

    def remote(src, dst, send_sem, recv_sem, target):
        return pltpu.make_async_remote_copy(
            src_ref=src,
            dst_ref=dst,
            send_sem=send_sem,
            recv_sem=recv_sem,
            device_id=target,
            device_id_type=MESH,
        )

    first = remote(orb_ref.at[0], pre, pre_s, pre_r, dev(hh=1 - h))
    first.start()

    def hand(t, block):
        src = buf.at[t, 2, block]
        for r, dk in ((0, t + 1), (1, -t - 1)):
            other = lax.rem(h + block, 2)
            if t == 0:
                other = jnp.where(lax.rem(k + r, 2) == 0, h, other)
            remote(
                src, buf.at[t, r, block], nb_s.at[t], nb_r.at[t, r], dev(dk, 0, other)
            ).start()

    def ag_edge(t, d, block, at, to, c=None):
        ref = buf.at[t, 2, block]
        whole = to not in GATHER_RELAYS
        i = slot_of(d, to)
        return remote(
            ref if whole else ref.at[c],
            ref if whole else ref.at[c],
            ag_s.at[t],
            ag_r.at[t, i, 0 if whole else c],
            dev(dz=(1 - 2 * d) * (to - at)),
        )

    def ag_pass(t, d, at, c):
        for to in GATHER_RELAYS:
            if to > at and parent(GATHER_RELAYS, to) == at:
                ag_edge(t, d, place(1 - d, at), at, to, c).start()

    def ag_leaves(t, d, at):
        for to in range(far, at, -1):
            if parent(GATHER_RELAYS, to) == at and to not in GATHER_RELAYS:
                ag_edge(t, d, place(1 - d, at), at, to).start()

    def ag_wait(t, d, at, c=None):
        ag_edge(t, d, place(1 - d, at), 0, at, c).wait_recv()

    def gather(t):
        last = 0
        for at in GATHER_RELAYS:
            if at > 0:

                @pl.loop(0, PIECES)
                def _(c):
                    for d in range(2):
                        ag_wait(t, d, at, c)
                        ag_pass(t, d, at, c)

            if at == GATHER_RELAYS[-1]:
                ag_edge(t, odd, place(1 - odd, at), at, half).start()
            for d in range(2):
                ag_leaves(t, d, at)
            for between in range(last + 1, at):
                for d in range(2):
                    ag_wait(t, d, between)
                    hand(t, place(1 - d, between))
            for d in range(2 if at > 0 else 1):
                hand(t, place(1 - d, at))
            last = at
        for between in range(last + 1, half):
            for d in range(2):
                ag_wait(t, d, between)
                hand(t, place(1 - d, between))
        ag_wait(t, 0, half)
        hand(t, place(0, half))

    def nb_wait(t, r):
        ref = buf.at[t, r]
        remote(ref, ref, nb_s.at[t], nb_r.at[t, r], dev(1)).wait_recv()

    def rs_copy(t, d, at, c, src):
        to = parent(REDUCE_RELAYS, at)
        i = slot_of(d, at)
        return remote(
            src,
            got.at[t, i, c],
            rs_s.at[t],
            rs_r.at[t, i, c],
            dev(dz=(1 - 2 * d) * (at - to)),
        )

    def rs_leaves(t, group):
        for c in range(PIECES):
            for at in group:
                if at == half:
                    rs_copy(t, odd, at, c, part.at[t, place(0, at), c]).start()
                else:
                    for d in range(2):
                        rs_copy(t, d, at, c, part.at[t, place(d, at), c]).start()

    leaves = [
        [at for at in range(half, 0, -1) if parent(REDUCE_RELAYS, at) == relay
         and at not in REDUCE_RELAYS]
        for relay in REDUCE_RELAYS[::-1]
    ]

    def rs_sum(t, d, at, c):
        total = part[t, place(d, at), c]
        for child in range(far, at, -1):
            if parent(REDUCE_RELAYS, child) == at:
                i = slot_of(d, child)
                rs_copy(t, d, child, c, got.at[t, i, c]).wait_recv()
                total = total + got[t, i, c]
        return total

    def rs_relay(t, at):
        i = REDUCE_RELAYS.index(at) - 1

        @pl.loop(0, PIECES)
        def _(c):
            sums = [rs_sum(t, d, at, c) for d in range(2)]
            if at == REDUCE_RELAYS[-1]:
                opposite = got.at[t, nz - 2, c]
                rs_copy(t, 0, half, c, opposite).wait_recv()
                add = opposite[...]
                none = jnp.zeros_like(add)
                sums[0] = sums[0] + jnp.where(odd == 0, add, none)
                sums[1] = sums[1] + jnp.where(odd == 1, add, none)
            for d in range(2):
                run[t, d, i, c] = sums[d]
                rs_copy(t, d, at, c, run.at[t, d, i, c]).start()

    def y_copy(t, c):
        return remote(
            ysend.at[t, c], yrecv.at[t, c], y_s.at[t], y_r.at[t, c], dev(hh=1 - h)
        )

    def reduce(t):
        for n, at in enumerate(REDUCE_RELAYS[:0:-1]):
            rs_relay(t, at)
            for leaf in leaves[n + 2 : n + 3]:
                rs_leaves(t, leaf)

        @pl.loop(0, PIECES)
        def _(c):
            total = rs_sum(t, 0, 0, c)
            for child in range(far, 0, -1):
                if parent(REDUCE_RELAYS, child) == 0:
                    i = slot_of(1, child)
                    rs_copy(t, 1, child, c, got.at[t, i, c]).wait_recv()
                    total = total + got[t, i, c]
            ysend[t, c] = total
            y_copy(t, c).start()

        @pl.loop(0, PIECES)
        def _(c):
            y_copy(t, c).wait_recv()
            total = ysend[t, c] + yrecv[t, c]
            here = pl.ds(pl.multiple_of(c * piece, piece), piece)
            ap[here, :] = total
            if t < STEPS - 1:
                fresh = c48[here, :] - UPDATE * (total * norm)
                c48[here, :] = fresh
                start(t + 1, c, fresh)

    def start(t, c, fresh):
        buf[t, 2, z, c] = fresh.astype(BF16)
        for d in range(2):
            ag_pass(t, d, 0, c)

    def half_of(which):
        return pl.ds(pl.multiple_of(which * (rows // 2), 8), rows // 2)

    tall = 768
    group = nz // 4
    for t in range(STEPS):
        if t == 0:
            first.wait_recv()
            c48[half_of(h), :] = orb_ref[0].astype(F32)
            c48[half_of(1 - h), :] = pre[...].astype(F32)
            for c in range(PIECES):
                start(0, c, c48[c * piece : (c + 1) * piece, :])
        gather(t)
        bt[...] = buf[t, 2].reshape(basis, cols).T
        if t == 0:
            fetch.wait()
        near = 1 - lax.rem(lax.div(k, t + 1), 2)
        for n in range(2):
            v = near if n == 0 else 1 - near
            nb_wait(t, v)
            slot = idx_ref[0, 2 * t + v]
            for p in range(2):

                @pl.loop(0, basis // tall)
                def _(i):
                    x = jnp.dot(
                        fit[slot, p, pl.ds(i * tall, tall), :],
                        buf[t, v].reshape(basis, cols),
                        preferred_element_type=F32,
                    )
                    at = (2 * n + p) * cols
                    xs[pl.ds(i * tall, tall), at : at + cols] = x.astype(BF16)

            pair = slice(2 * n * cols, 2 * (n + 1) * cols)
            mt[:, pair] = jnp.dot(
                bt[...], xs[:, pair], preferred_element_type=F32
            ).astype(BF16)

        home = lax.div(z, group) + 2
        side = jnp.where(lax.rem(z, group) * 2 >= group, 1, 3)

        def tile(i):
            y = lax.dot_general(
                xs[pl.ds(pl.multiple_of(i * (basis // 4), basis // 4), basis // 4), :],
                mt[...],
                (((1,), (1,)), ((), ())),
                preferred_element_type=F32,
            )
            part[t, pl.ds(i * group, group)] = y.reshape(group, PIECES, piece, cols)

        @pl.loop(0, 2)
        def _(i):
            tile(lax.rem(home + i * side, 4))

        rs_leaves(t, leaves[0])

        @pl.loop(0, 2)
        def _(i):
            tile(lax.rem(home + 2 + i * side, 4))

        rs_leaves(t, leaves[1])
        reduce(t)
        tot_ref[t] = ap[half_of(h), :]

    first.wait_send()
    for t in range(STEPS):
        y_all = ysend.at[t]
        remote(y_all, y_all, y_s.at[t], y_r.at[t, 0], dev(1)).wait_send()
        ring = buf.at[t, 2, pl.ds(0, nz - 1)]
        remote(ring, ring, ag_s.at[t], ag_r.at[t, 0, 0], dev(1)).wait_send()
        handed = buf.at[t, pl.ds(0, 2)]
        remote(handed, handed, nb_s.at[t], nb_r.at[t, 0], dev(1)).wait_send()
        summed = got.at[t]
        remote(summed, summed, rs_s.at[t], rs_r.at[t, 0, 0], dev(1)).wait_send()


def finish(norm, tot_ref, orb_ref, ex_ref, out_ref):
    current = orb_ref[0].astype(F32)
    for t in range(STEPS):
        applied = tot_ref[t] * norm
        ex_ref[t, 0] = applied
        current = current - UPDATE * applied
    out_ref[0] = current


def on_device(orbitals, fitted, kpoint_pair_index):
    _, half, cols = orbitals.shape
    _, slots, layers, basis, _ = fitted.shape
    na = lax.axis_size("aux")
    nz, rows = na // 2, 2 * half
    piece = rows // PIECES
    norm = 1.0 / (layers * na * cols)
    relays = len(REDUCE_RELAYS) - 1
    vmem = functools.partial(pl.BlockSpec, memory_space=pltpu.VMEM)
    dma = pltpu.SemaphoreType.DMA
    totals = pl.pallas_call(
        functools.partial(kernel, norm),
        out_shape=jax.ShapeDtypeStruct((STEPS, half, cols), F32),
        in_specs=[
            vmem(),
            pl.BlockSpec(memory_space=pl.ANY),
            pl.BlockSpec(memory_space=pltpu.SMEM),
        ],
        out_specs=vmem(),
        scratch_shapes=[
            pltpu.VMEM((slots, layers, basis, basis), BF16),
            pltpu.VMEM((half, cols), BF16),
            pltpu.VMEM((rows, cols), F32),
            pltpu.VMEM((STEPS, 3, nz, PIECES, piece, cols), BF16),
            pltpu.VMEM((basis, 4 * cols), BF16),
            pltpu.VMEM((cols, basis), BF16),
            pltpu.VMEM((cols, 4 * cols), BF16),
            pltpu.VMEM((STEPS, nz, PIECES, piece, cols), F32),
            pltpu.VMEM((STEPS, 2, relays, PIECES, piece, cols), F32),
            pltpu.VMEM((STEPS, nz - 1, PIECES, piece, cols), F32),
            pltpu.VMEM((STEPS, PIECES, piece, cols), F32),
            pltpu.VMEM((STEPS, PIECES, piece, cols), F32),
            pltpu.VMEM((rows, cols), F32),
            dma,
            dma,
            dma,
            dma((STEPS,)),
            dma((STEPS, 2)),
            dma((STEPS,)),
            dma((STEPS, nz - 1, PIECES)),
            dma((STEPS,)),
            dma((STEPS, nz - 1, PIECES)),
            dma((STEPS,)),
            dma((STEPS, PIECES)),
        ],
        compiler_params=pltpu.CompilerParams(
            collective_id=0, has_side_effects=True, vmem_limit_bytes=56 * 2**20
        ),
        name="exchange",
    )(orbitals, fitted, kpoint_pair_index)
    return pl.pallas_call(
        functools.partial(finish, norm),
        out_shape=(
            jax.ShapeDtypeStruct((STEPS, 1, half, cols), F32),
            jax.ShapeDtypeStruct((1, half, cols), F32),
        ),
        in_specs=[vmem(), vmem()],
        out_specs=(vmem(), vmem()),
        name="finish",
    )(totals, orbitals)


def solution(mesh):
    placed = (P("kpt", "aux", None), P("kpt", None, "aux", None, None), P("kpt", None))
    return jax.shard_map(
        on_device,
        mesh=mesh,
        in_specs=placed,
        out_specs=(P(None, "kpt", "aux", None), P("kpt", "aux", None)),
        check_vma=False,
    )
```
